32 devices in a mesh: row: 4 (over z), col: 8 (over y, x, core).
Axes of the slice: x: 2, y: 2, z: 4, core: 2. Of those that a mesh axis runs over, the one named last changes fastest.
Arguments:
- object_amplitude: float32 [1024, 2048], P('row', 'col'), may hold values from 0.3 to 3
- object_phase: float32 [1024, 2048], P('row', 'col'), may hold values from -3.140625 to 3.140625
- probe: float32 [4, 2, 256, 256], replicated, may hold values from -6 to 6
- amplitudes: float32 [256, 256, 256], P(('row', 'col')), may hold values from 0.5 to 3
- positions: int32 [256, 2], P(('row', 'col')), may hold values from -64 to 64
Outputs:
- new_object: float32 [2, 1024, 2048], P(None, 'row', 'col')
- new_probe: float32 [4, 2, 256, 256], replicated
The draws below stay inside these ranges and needn't reach their ends.
Inputs may be any that keep to these rules, and one draw needn't show every extreme that they name: `positions`: row and column offsets of each frame's first pixel from the first pixel of its owner tile f // 8, tiles row-major; both ends of the range occur.
All inputs are finite; a program needn't handle non-finite values.
Results may differ from the reference program's by a relative error of at most 0.0014.
The reference program's roundings to bfloat16 on the way count: a program that leaves them out, or rounds other values in their place, can miss the bound.
Values sent between devices are 32-bit elements; how exact they have to be, the bound alone decides.
A program may use at most 192 MiB of HBM per device.

```python
import math
import jax
import jax.numpy as jnp
from jax import lax

P_SIZE = 256
MODES = 4
TILE = 256
H = 64
FR_DEV = 8
FRAMES = 256
NYO = 1024
NXO = 2048
N_ROW = 4
N_COL = 8


def place_ends(array, stream_key, low, top_value):
    longest = array.shape.index(max(array.shape))
    spots = []
    for shift in (0, 1):
        where = [jax.random.randint(jax.random.fold_in(stream_key, axis), (), 0, length) for axis, length in enumerate(array.shape)]
        where[longest] = (where[longest] + shift) % array.shape[longest]
        spots.append(tuple(where))
    return array.at[spots[0]].set(low).at[spots[1]].set(top_value)


def levels(stream_key, dims, shards, low, high):
    def one(axis_at, parts):
        steps = jax.random.uniform(jax.random.fold_in(jax.random.fold_in(stream_key, 6), axis_at), (parts,), jnp.float32, low / len(shards), high / len(shards))
        return jnp.repeat(jnp.exp(steps), dims[axis_at] // parts).reshape((-1,) + (1,) * (len(dims) - axis_at - 1))

    loudness = one(*shards[0])
    for cut in shards[1:]:
        loudness = loudness * one(*cut)
    return loudness


def centred(rng, dims, spread, reach, held_as=jnp.bfloat16):
    return jnp.clip(spread * jax.random.normal(rng, dims, jnp.float32), -reach, reach).astype(held_as)


def setup_inputs(seed: int = 0) -> dict:
    seeds = jax.random.split(jax.random.key(seed), 6)
    object_amplitude = jnp.clip(jnp.exp(math.log(3.0) - 2.3025851 * jax.random.uniform(seeds[0], (NYO, NXO), jnp.float32) ** levels(seeds[0], (NYO, NXO), ((0, 4), (1, 8)), -0.2, 0.2)), 0.3, 3.0)
    object_phase = jnp.clip(jax.random.uniform(seeds[1], (NYO, NXO), jnp.float32, -3.140625, 3.140625), -3.140625, 3.140625)
    probe = centred(seeds[2], (MODES, 2, P_SIZE, P_SIZE), 1.0, 6.0, jnp.float32)
    amplitudes = jnp.clip(0.5 + 2.5 * jax.random.uniform(seeds[3], (FRAMES, P_SIZE, P_SIZE), jnp.float32) ** levels(seeds[3], (FRAMES, P_SIZE, P_SIZE), ((0, 32),), -0.2, 0.2), 0.5, 3.0)
    positions = place_ends(jax.random.randint(seeds[4], (FRAMES, 2), 0 - H, TILE - P_SIZE + H + 1), jax.random.fold_in(seeds[4], 1), 0 - H, TILE - P_SIZE + H).astype(jnp.int32)
    return dict(object_amplitude=object_amplitude, object_phase=object_phase, probe=probe, amplitudes=amplitudes, positions=positions)


def fourier_table(frame_side, exponent_sign):
    counter = jnp.arange(frame_side, dtype=jnp.int32)
    product = counter[:, None] * counter[None, :] % frame_side
    phase_angle = product.astype(jnp.float32) * (2.0 * math.pi / frame_side)
    norming = 1.0 / math.sqrt(frame_side)
    real_part = jnp.cos(phase_angle) * norming
    imaginary = exponent_sign * jnp.sin(phase_angle) * norming
    upper_rows = jnp.stack([real_part, -imaginary], axis=1)
    lower_rows = jnp.stack([imaginary, real_part], axis=1)
    return jnp.stack([upper_rows, lower_rows], axis=0).astype(jnp.bfloat16)

def transform(matrix, values):
    wide = matrix.astype(jnp.float32)
    halfway = jnp.einsum('akcy,fmcyx->fmakx', wide, values.astype(jnp.float32), precision=lax.Precision.HIGHEST)
    halfway = lax.optimization_barrier(halfway.astype(jnp.bfloat16)).astype(jnp.float32)
    return jnp.einsum('fmakx,blax->fmbkl', halfway, wide, precision=lax.Precision.HIGHEST)

def frame_terms(patches, probe, measured, forward, inverse):
    object_real = patches[:, None, 0]
    object_imag = patches[:, None, 1]
    probe_real = probe[None, :, 0]
    probe_imag = probe[None, :, 1]
    exit_wave = jnp.stack([probe_real * object_real - probe_imag * object_imag, probe_real * object_imag + probe_imag * object_real], axis=2)
    spectrum = transform(forward, exit_wave.astype(jnp.bfloat16))
    intensity = lax.optimization_barrier(jnp.sum(spectrum * spectrum, axis=(1, 2)))
    factor = measured / jnp.maximum(jnp.sqrt(intensity), 1.0)
    corrected = (spectrum * factor[:, None, None]).astype(jnp.bfloat16)
    returned = transform(inverse, corrected)
    change = returned - exit_wave
    change_real = change[:, :, 0]
    change_imag = change[:, :, 1]
    object_gradient = jnp.stack([lax.optimization_barrier(jnp.sum(probe_real * change_real + probe_imag * change_imag, axis=1)), lax.optimization_barrier(jnp.sum(probe_real * change_imag - probe_imag * change_real, axis=1))], axis=1)
    probe_gradient = jnp.stack([lax.optimization_barrier(jnp.sum(object_real * change_real + object_imag * change_imag, axis=0)), lax.optimization_barrier(jnp.sum(object_real * change_imag - object_imag * change_real, axis=0))], axis=1)
    weight = lax.optimization_barrier(jnp.sum(patches * patches, axis=(0, 1)))
    return (object_gradient, probe_gradient, weight)

def reference(object_amplitude, object_phase, probe, amplitudes, positions):
    object_field = jnp.stack([object_amplitude * jnp.cos(object_phase), object_amplitude * jnp.sin(object_phase)])
    padded = jnp.pad(object_field, ((0, 0), (H, H), (H, H)))
    forward = fourier_table(P_SIZE, -1.0)
    inverse = fourier_table(P_SIZE, 1.0)
    blocks = N_ROW * N_COL
    measured_all = amplitudes.reshape(blocks, FR_DEV, P_SIZE, P_SIZE)
    offsets_all = positions.reshape(blocks, FR_DEV, 2)

    def one_block(running, inputs_here):
        gradient_sum, probe_total, weight_total = running
        block_index, measured, offsets = inputs_here
        tile_row = block_index // N_COL
        tile_col = block_index % N_COL
        anchor = jnp.stack([tile_row * TILE + H, tile_col * TILE + H]).astype(jnp.int32)
        starts = (offsets + anchor[None, :]).astype(jnp.int32)
        patches = jax.vmap(lambda start_pair: lax.dynamic_slice(padded, (jnp.int32(0), start_pair[0], start_pair[1]), (2, P_SIZE, P_SIZE)))(starts)
        object_gradient, probe_gradient, weight = frame_terms(patches, probe, measured, forward, inverse)

        def place_frame(counter, canvas):
            corner = starts[counter]
            current = lax.dynamic_slice(canvas, (jnp.int32(0), corner[0], corner[1]), (2, P_SIZE, P_SIZE))
            return lax.dynamic_update_slice(canvas, current + object_gradient[counter], (jnp.int32(0), corner[0], corner[1]))
        gradient_sum = lax.fori_loop(0, FR_DEV, place_frame, gradient_sum)
        return ((gradient_sum, probe_total + probe_gradient, weight_total + weight), None)
    initial = (jnp.zeros_like(padded), jnp.zeros((MODES, 2, P_SIZE, P_SIZE), jnp.float32), jnp.zeros((P_SIZE, P_SIZE), jnp.float32))
    (gradient_sum, probe_total, weight_total), unused = lax.scan(one_block, initial, (jnp.arange(blocks, dtype=jnp.int32), measured_all, offsets_all))
    new_probe = probe + probe_total / (weight_total + 1e-05)
    step_size = 1.0 / (jnp.max(lax.optimization_barrier(jnp.sum(probe * probe, axis=(0, 1)))) + 1e-06)
    new_object = object_field + gradient_sum[:, H:H + NYO, H:H + NXO] * step_size
    return (new_object, new_probe)
```

```python
import math

import jax
import jax.numpy as jnp
from jax import lax
from jax.experimental import pallas as pl
from jax.experimental.pallas import tpu as pltpu
from jax.sharding import PartitionSpec as P

H = 64


def extended_2(block, sides, width):
    for axis, dim in sides:
        count = lax.axis_size(axis)
        forward = [(i, i + 1) for i in range(count - 1)]
        backward = [(target, source) for source, target in forward]
        low = lax.ppermute(
            lax.slice_in_dim(block, block.shape[dim] - width, None, axis=dim), axis, forward
        )
        high = lax.ppermute(lax.slice_in_dim(block, 0, width, axis=dim), axis, backward)
        block = jnp.concatenate([low, block, high], axis=dim)
    return block


def fourier_tables(side, sign):
    counter = jnp.arange(side, dtype=jnp.int32)
    product = counter[:, None] * counter[None, :] % side
    angle = product.astype(jnp.float32) * (2.0 * math.pi / side)
    norming = 1.0 / math.sqrt(side)
    real = (jnp.cos(angle) * norming).astype(jnp.bfloat16)
    imag = (sign * jnp.sin(angle) * norming).astype(jnp.bfloat16)
    left = jnp.concatenate(
        [jnp.concatenate([real, -imag], axis=1), jnp.concatenate([imag, real], axis=1)], axis=0
    )
    right = jnp.concatenate(
        [jnp.concatenate([real, imag], axis=1), jnp.concatenate([-imag, real], axis=1)], axis=0
    )
    return left, right


def dot(a, b):
    return jnp.dot(a, b, preferred_element_type=jnp.float32)


def frames_kernel(
    pos_ref, ext_ref, probe_ref, amp_ref, fl_ref, fr_ref, il_ref, ir_ref,
    canvas_ref, s_ref, w_ref,
    o_scr, x_scr, h_scr, spec_scr, int_scr, p2_scr, g_scr,
):
    frame = pl.program_id(0)
    modes, _, n, _ = probe_ref.shape
    wide = ext_ref.shape[2]
    step = 32
    chunks = [pl.ds(r, step) for r in range(0, n, step)]
    low = [pl.ds(n + r, step) for r in range(0, n, step)]

    @pl.when(frame == 0)
    def _():
        canvas_ref[...] = jnp.zeros_like(canvas_ref)
        s_ref[...] = jnp.zeros_like(s_ref)
        w_ref[...] = jnp.zeros_like(w_ref)
        for rows in chunks:
            total = jnp.zeros((step, n), jnp.float32)
            for m in range(modes):
                for c in range(2):
                    total += probe_ref[m, c, rows, :] * probe_ref[m, c, rows, :]
            p2_scr[rows, :] = total

    r0 = pos_ref[frame, 0] + H
    c0 = pos_ref[frame, 1] + H
    base = pl.multiple_of(r0 // 8 * 8, 8)
    off = r0 - base
    tall = 64
    for r in range(0, n, tall):
        rows = pl.ds(r, tall)
        weight = w_ref[rows, :]
        for c in range(2):
            part = ext_ref[c, pl.ds(base + r, tall + 8), :]
            part = pltpu.roll(part, lax.rem(wide - c0, wide), axis=1)[:, :n]
            part = pltpu.roll(part, lax.rem(tall + 8 - off, tall + 8), axis=0)[:tall]
            o_scr[c, rows, :] = part
            weight += part * part
        w_ref[rows, :] = weight

    for m in range(modes):
        for rows, under in zip(chunks, low):
            pr, pi = probe_ref[m, 0, rows, :], probe_ref[m, 1, rows, :]
            o_r, o_i = o_scr[0, rows, :], o_scr[1, rows, :]
            x_scr[m, rows, :] = (pr * o_r - pi * o_i).astype(jnp.bfloat16)
            x_scr[m, under, :] = (pr * o_i + pi * o_r).astype(jnp.bfloat16)
        half = dot(fl_ref[...], x_scr[m]).astype(jnp.bfloat16)
        h_scr[m, :, :n] = half[:n]
        h_scr[m, :, n:] = half[n:]
        spec_scr[m] = dot(h_scr[m], fr_ref[...])

    for rows in chunks:
        total = jnp.zeros((step, n), jnp.float32)
        for m in range(modes):
            a, b = spec_scr[m, rows, :n], spec_scr[m, rows, n:]
            total += a * a + b * b
        int_scr[rows, :] = amp_ref[0, rows, :] / jnp.maximum(jnp.sqrt(total), 1.0)

    for m in range(modes):
        for rows, under in zip(chunks, low):
            fac = int_scr[rows, :]
            x_scr[m, rows, :] = (spec_scr[m, rows, :n] * fac).astype(jnp.bfloat16)
            x_scr[m, under, :] = (spec_scr[m, rows, n:] * fac).astype(jnp.bfloat16)
        half = dot(il_ref[...], x_scr[m]).astype(jnp.bfloat16)
        h_scr[m, :, :n] = half[:n]
        h_scr[m, :, n:] = half[n:]
        spec_scr[m] = dot(h_scr[m], ir_ref[...])
        for rows in chunks:
            br, bi = spec_scr[m, rows, :n], spec_scr[m, rows, n:]
            o_r, o_i = o_scr[0, rows, :], o_scr[1, rows, :]
            pr, pi = probe_ref[m, 0, rows, :], probe_ref[m, 1, rows, :]
            s_ref[m, 0, rows, :] += o_r * br + o_i * bi
            s_ref[m, 1, rows, :] += o_r * bi - o_i * br
            gr = pr * br + pi * bi
            gi = pr * bi - pi * br
            if m == 0:
                p2 = p2_scr[rows, :]
                gr -= o_r * p2
                gi -= o_i * p2
            else:
                gr += g_scr[0, rows, :]
                gi += g_scr[1, rows, :]
            g_scr[0, rows, :] = gr
            g_scr[1, rows, :] = gi

    for r in range(0, n, tall):
        for c in range(2):
            part = jnp.concatenate(
                [g_scr[c, pl.ds(r, tall), :], jnp.zeros((8, n), jnp.float32)], axis=0
            )
            part = pltpu.roll(part, off, axis=0)
            part = jnp.concatenate([part, jnp.zeros((tall + 8, wide - n), jnp.float32)], axis=1)
            canvas_ref[c, pl.ds(base + r, tall + 8), :] += pltpu.roll(part, c0, axis=1)


def frame_terms(positions, extended, probe, amplitudes):
    modes, _, n, _ = probe.shape
    frames = amplitudes.shape[0]
    wide = extended.shape[2]
    high = extended.shape[1]
    forward = fourier_tables(n, -1.0)
    inverse = fourier_tables(n, 1.0)
    f32 = jnp.float32

    def whole(shape):
        return pl.BlockSpec(shape, lambda i, pos: (0,) * len(shape))

    return pl.pallas_call(
        frames_kernel,
        grid_spec=pltpu.PrefetchScalarGridSpec(
            num_scalar_prefetch=1,
            grid=(frames,),
            in_specs=[
                whole(extended.shape),
                whole(probe.shape),
                pl.BlockSpec((1, n, n), lambda i, pos: (i, 0, 0)),
            ]
            + [whole((2 * n, 2 * n))] * 4,
            out_specs=[whole((2, high, wide)), whole(probe.shape), whole((n, n))],
            scratch_shapes=[
                pltpu.VMEM((2, n, n), f32),
                pltpu.VMEM((modes, 2 * n, n), jnp.bfloat16),
                pltpu.VMEM((modes, n, 2 * n), jnp.bfloat16),
                pltpu.VMEM((modes, n, 2 * n), f32),
                pltpu.VMEM((n, n), f32),
                pltpu.VMEM((n, n), f32),
                pltpu.VMEM((2, n, n), f32),
            ],
        ),
        out_shape=[
            jax.ShapeDtypeStruct((2, high, wide), f32),
            jax.ShapeDtypeStruct(probe.shape, f32),
            jax.ShapeDtypeStruct((n, n), f32),
        ],
        compiler_params=pltpu.CompilerParams(vmem_limit_bytes=48 * 1024 * 1024),
        name="frames",
    )(positions, extended, probe, amplitudes, *forward, *inverse)


def shards(object_amplitude, object_phase, probe, amplitudes, positions):
    tile_side = object_amplitude.shape[0]
    object_field = jnp.stack(
        [object_amplitude * jnp.cos(object_phase), object_amplitude * jnp.sin(object_phase)]
    )
    extended = extended_2(object_field, (("row", 1), ("col", 2)), H)
    extended = jnp.pad(extended, ((0, 0), (0, 8), (0, 0)))
    canvas, probe_sum, weight = frame_terms(positions, extended, probe, amplitudes)
    canvas = canvas[:, : tile_side + 2 * H]
    row_edges = jnp.concatenate([canvas[:, :H], canvas[:, tile_side + H :]], axis=1)
    from_rows = extended_2(row_edges, (("row", 1),), H)
    canvas = canvas.at[:, H : 2 * H].add(from_rows[:, :H])
    canvas = canvas.at[:, tile_side : tile_side + H].add(from_rows[:, 3 * H :])
    middle = canvas[:, H : tile_side + H]
    col_edges = jnp.concatenate([middle[:, :, :H], middle[:, :, tile_side + H :]], axis=2)
    from_cols = extended_2(col_edges, (("col", 2),), H)
    inner = middle[:, :, H : tile_side + H]
    inner = inner.at[:, :, :H].add(from_cols[:, :, :H])
    inner = inner.at[:, :, tile_side - H :].add(from_cols[:, :, 3 * H :])
    step_size = 1.0 / (jnp.max(jnp.sum(probe * probe, axis=(0, 1))) + 1e-06)
    new_object = object_field + inner * step_size
    total_sum, total_weight = lax.psum((probe_sum, weight), ("row", "col"))
    new_probe = probe + (total_sum - probe * total_weight) / (total_weight + 1e-05)
    return (new_object, new_probe)


def solution(mesh):
    in_specs = (
        P("row", "col"),
        P("row", "col"),
        P(),
        P(("row", "col"), None, None),
        P(("row", "col"), None),
    )
    out_specs = (P(None, "row", "col"), P())
    return jax.shard_map(shards, mesh=mesh, in_specs=in_specs, out_specs=out_specs, check_vma=False)
```

```python
import functools
import math

import jax
import jax.numpy as jnp
from jax import lax
from jax.experimental import pallas as pl
from jax.experimental.pallas import tpu as pltpu
from jax.sharding import PartitionSpec as P

H = 64


def extended_2(block, sides, width):
    for axis, dim in sides:
        count = lax.axis_size(axis)
        forward = [(i, i + 1) for i in range(count - 1)]
        backward = [(target, source) for source, target in forward]
        low = lax.ppermute(
            lax.slice_in_dim(block, block.shape[dim] - width, None, axis=dim), axis, forward
        )
        high = lax.ppermute(lax.slice_in_dim(block, 0, width, axis=dim), axis, backward)
        block = jnp.concatenate([low, block, high], axis=dim)
    return block


def fourier_tables(side, sign):
    counter = jnp.arange(side, dtype=jnp.int32)
    product = counter[:, None] * counter[None, :] % side
    angle = product.astype(jnp.float32) * (2.0 * math.pi / side)
    norming = 1.0 / math.sqrt(side)
    real = (jnp.cos(angle) * norming).astype(jnp.bfloat16)
    imag = (sign * jnp.sin(angle) * norming).astype(jnp.bfloat16)
    left = jnp.concatenate(
        [jnp.concatenate([real, -imag], axis=1), jnp.concatenate([imag, real], axis=1)], axis=0
    )
    right = jnp.concatenate(
        [jnp.concatenate([real, imag], axis=1), jnp.concatenate([-imag, real], axis=1)], axis=0
    )
    return left, right


def dot(a, b):
    return jnp.dot(a, b, preferred_element_type=jnp.float32)


def frames_kernel(
    pos_ref, ext_ref, probe_ref, amp_ref, fl_ref, fr_ref, il_ref, ir_ref,
    canvas_ref, s_ref,
    o_scr, x_scr, h_scr, spec_scr, int_scr, p2_scr, g_scr,
):
    frame = pl.program_id(0)
    modes, _, n, _ = probe_ref.shape
    wide = ext_ref.shape[2]
    step = 32
    lanes = n // 2
    planes = 2 * modes

    def add_sum(plane, rows, value):
        s_ref[0, plane, rows, :] += value[:, :lanes]
        s_ref[1, plane, rows, :] += value[:, lanes:]

    chunks = [pl.ds(r, step) for r in range(0, n, step)]
    low = [pl.ds(n + r, step) for r in range(0, n, step)]

    @pl.when(frame == 0)
    def _():
        canvas_ref[...] = jnp.zeros_like(canvas_ref)
        s_ref[...] = jnp.zeros_like(s_ref)
        for rows in chunks:
            total = jnp.zeros((step, n), jnp.float32)
            for m in range(modes):
                for c in range(2):
                    total += probe_ref[m, c, rows, :] * probe_ref[m, c, rows, :]
            p2_scr[rows, :] = total

    r0 = pos_ref[frame, 0] + H
    c0 = pos_ref[frame, 1] + H
    base = pl.multiple_of(r0 // 8 * 8, 8)
    off = r0 - base
    tall = 64
    for r in range(0, n, tall):
        rows = pl.ds(r, tall)
        weight = jnp.zeros((tall, n), jnp.float32)
        for c in range(2):
            part = ext_ref[c, pl.ds(base + r, tall + 8), :]
            part = pltpu.roll(part, lax.rem(wide - c0, wide), axis=1)[:, :n]
            part = pltpu.roll(part, lax.rem(tall + 8 - off, tall + 8), axis=0)[:tall]
            o_scr[c, rows, :] = part
            weight += part * part
        add_sum(planes, rows, weight)

    for m in range(modes):
        for rows, under in zip(chunks, low):
            pr, pi = probe_ref[m, 0, rows, :], probe_ref[m, 1, rows, :]
            o_r, o_i = o_scr[0, rows, :], o_scr[1, rows, :]
            x_scr[m, rows, :] = (pr * o_r - pi * o_i).astype(jnp.bfloat16)
            x_scr[m, under, :] = (pr * o_i + pi * o_r).astype(jnp.bfloat16)
        half = dot(fl_ref[...], x_scr[m]).astype(jnp.bfloat16)
        h_scr[m, :, :n] = half[:n]
        h_scr[m, :, n:] = half[n:]
        spec_scr[m] = dot(h_scr[m], fr_ref[...])

    for rows in chunks:
        total = jnp.zeros((step, n), jnp.float32)
        for m in range(modes):
            a, b = spec_scr[m, rows, :n], spec_scr[m, rows, n:]
            total += a * a + b * b
        int_scr[rows, :] = amp_ref[0, rows, :] / jnp.maximum(jnp.sqrt(total), 1.0)

    for m in range(modes):
        for rows, under in zip(chunks, low):
            fac = int_scr[rows, :]
            x_scr[m, rows, :] = (spec_scr[m, rows, :n] * fac).astype(jnp.bfloat16)
            x_scr[m, under, :] = (spec_scr[m, rows, n:] * fac).astype(jnp.bfloat16)
        half = dot(il_ref[...], x_scr[m]).astype(jnp.bfloat16)
        h_scr[m, :, :n] = half[:n]
        h_scr[m, :, n:] = half[n:]
        spec_scr[m] = dot(h_scr[m], ir_ref[...])
        for rows in chunks:
            br, bi = spec_scr[m, rows, :n], spec_scr[m, rows, n:]
            o_r, o_i = o_scr[0, rows, :], o_scr[1, rows, :]
            pr, pi = probe_ref[m, 0, rows, :], probe_ref[m, 1, rows, :]
            add_sum(2 * m, rows, o_r * br + o_i * bi)
            add_sum(2 * m + 1, rows, o_r * bi - o_i * br)
            gr = pr * br + pi * bi
            gi = pr * bi - pi * br
            if m == 0:
                p2 = p2_scr[rows, :]
                gr -= o_r * p2
                gi -= o_i * p2
            else:
                gr += g_scr[0, rows, :]
                gi += g_scr[1, rows, :]
            g_scr[0, rows, :] = gr
            g_scr[1, rows, :] = gi

    for r in range(0, n, tall):
        for c in range(2):
            part = jnp.concatenate(
                [g_scr[c, pl.ds(r, tall), :], jnp.zeros((8, n), jnp.float32)], axis=0
            )
            part = pltpu.roll(part, off, axis=0)
            part = jnp.concatenate([part, jnp.zeros((tall + 8, wide - n), jnp.float32)], axis=1)
            canvas_ref[c, pl.ds(base + r, tall + 8), :] += pltpu.roll(part, c0, axis=1)


def frame_terms(positions, extended, probe, amplitudes):
    modes, _, n, _ = probe.shape
    frames = amplitudes.shape[0]
    wide = extended.shape[2]
    high = extended.shape[1]
    forward = fourier_tables(n, -1.0)
    inverse = fourier_tables(n, 1.0)
    f32 = jnp.float32
    sums = (2, 2 * modes + 1, n, n // 2)

    def whole(shape):
        return pl.BlockSpec(shape, lambda i, pos: (0,) * len(shape))

    return pl.pallas_call(
        frames_kernel,
        grid_spec=pltpu.PrefetchScalarGridSpec(
            num_scalar_prefetch=1,
            grid=(frames,),
            in_specs=[
                whole(extended.shape),
                whole(probe.shape),
                pl.BlockSpec((1, n, n), lambda i, pos: (i, 0, 0)),
            ]
            + [whole((2 * n, 2 * n))] * 4,
            out_specs=[whole((2, high, wide)), whole(sums)],
            scratch_shapes=[
                pltpu.VMEM((2, n, n), f32),
                pltpu.VMEM((modes, 2 * n, n), jnp.bfloat16),
                pltpu.VMEM((modes, n, 2 * n), jnp.bfloat16),
                pltpu.VMEM((modes, n, 2 * n), f32),
                pltpu.VMEM((n, n), f32),
                pltpu.VMEM((n, n), f32),
                pltpu.VMEM((2, n, n), f32),
            ],
        ),
        out_shape=[
            jax.ShapeDtypeStruct((2, high, wide), f32),
            jax.ShapeDtypeStruct(sums, f32),
        ],
        compiler_params=pltpu.CompilerParams(vmem_limit_bytes=48 * 1024 * 1024),
        name="frames",
    )(positions, extended, probe, amplitudes, *forward, *inverse)


def plan(sizes, rows):
    bits = [[(axis, b) for b in range(size.bit_length() - 1)] for axis, size in sizes]
    row_bits, col_bits = bits
    rest = col_bits[1:]
    cut = len(rest) // 2
    orders = [col_bits[:1] + rest + row_bits, col_bits[:1] + rest[cut:] + rest[:cut] + row_bits]
    plans = []
    for order in orders:
        left, stages, offset = rows, [], 0
        for axis, bit in order:
            halved = left > 8
            left = left // 2 if halved else left
            stages.append((axis, bit, halved, left, offset))
            offset += left
        plans.append(stages)
    return plans, max(stages[-1][3] + stages[-1][4] for stages in plans)


def total_kernel(plans, in_ref, out_ref, partial, landed, send_rs, recv_rs, send_ag, recv_ag):
    coords = {"row": lax.axis_index("row"), "col": lax.axis_index("col")}

    def bit_of(axis, bit):
        return lax.rem(coords[axis] // (1 << bit), 2)

    def partner(axis, bit):
        flipped = dict(coords)
        flipped[axis] = coords[axis] + (1 - 2 * bit_of(axis, bit)) * (1 << bit)
        return (flipped["row"], flipped["col"])

    barrier = pltpu.get_barrier_semaphore()
    for axis, bit, *_ in plans[0]:
        pl.semaphore_signal(
            barrier, inc=1, device_id=partner(axis, bit), device_id_type=pl.DeviceIdType.MESH
        )
    pl.semaphore_wait(barrier, len(plans[0]))

    count = len(plans[0])
    starts = [[0], [0]]
    flights = [None, None]

    def send(part, stage):
        axis, bit, halved, size, offset = plans[part][stage]
        start = starts[part][-1]
        mine = bit_of(axis, bit)
        source = in_ref if stage == 0 else partial
        gone = pl.multiple_of(start + (1 - mine) * size, 8) if halved else start
        kept = pl.multiple_of(start + mine * size, 8) if halved else start
        starts[part].append(kept)
        copy = pltpu.make_async_remote_copy(
            src_ref=source.at[part, :, pl.ds(gone, size), :],
            dst_ref=landed.at[part, :, pl.ds(offset, size), :],
            send_sem=send_rs.at[part, stage],
            recv_sem=recv_rs.at[part, stage],
            device_id=partner(axis, bit),
            device_id_type=pl.DeviceIdType.MESH,
        )
        copy.start()
        flights[part] = copy

    def take(part, stage):
        _, _, _, size, offset = plans[part][stage]
        flights[part].wait()
        source = in_ref if stage == 0 else partial
        rows = pl.ds(starts[part][-1], size)
        target = out_ref if stage == count - 1 else partial
        target[part, :, rows, :] = (
            source[part, :, rows, :] + landed[part, :, pl.ds(offset, size), :]
        )

    def spread(part, stage):
        axis, bit, halved, size, _ = plans[part][stage]
        flights[part] = None
        if not halved:
            return
        rows = pl.ds(starts[part][stage + 1], size)
        copy = pltpu.make_async_remote_copy(
            src_ref=out_ref.at[part, :, rows, :],
            dst_ref=out_ref.at[part, :, rows, :],
            send_sem=send_ag.at[part, stage],
            recv_sem=recv_ag.at[part, stage],
            device_id=partner(axis, bit),
            device_id_type=pl.DeviceIdType.MESH,
        )
        copy.start()
        flights[part] = copy

    for part in range(2):
        send(part, 0)
    for stage in range(count):
        for part in range(2):
            take(part, stage)
            if stage + 1 < count:
                send(part, stage + 1)
            else:
                spread(part, stage)
    for stage in range(count - 2, -2, -1):
        for part in range(2):
            if flights[part] is not None:
                flights[part].wait()
            if stage >= 0:
                spread(part, stage)


def total_over_mesh(values):
    sizes = [(axis, lax.axis_size(axis)) for axis in ("row", "col")]
    parts, planes, rows, lanes = values.shape
    plans, landing = plan(sizes, rows)
    count = len(plans[0])
    dma = pltpu.SemaphoreType.DMA((parts, count))
    return pl.pallas_call(
        functools.partial(total_kernel, plans),
        out_shape=jax.ShapeDtypeStruct(values.shape, values.dtype),
        in_specs=[pl.BlockSpec(memory_space=pltpu.VMEM)],
        out_specs=pl.BlockSpec(memory_space=pltpu.VMEM),
        scratch_shapes=[
            pltpu.VMEM(values.shape, values.dtype),
            pltpu.VMEM((parts, planes, landing, lanes), values.dtype),
            dma, dma, dma, dma,
        ],
        compiler_params=pltpu.CompilerParams(
            collective_id=0, has_side_effects=True, vmem_limit_bytes=24 * 1024 * 1024
        ),
        name="total",
    )(values)


def shards(object_amplitude, object_phase, probe, amplitudes, positions):
    tile_side = object_amplitude.shape[0]
    object_field = jnp.stack(
        [object_amplitude * jnp.cos(object_phase), object_amplitude * jnp.sin(object_phase)]
    )
    extended = extended_2(object_field, (("row", 1), ("col", 2)), H)
    extended = jnp.pad(extended, ((0, 0), (0, 8), (0, 0)))
    canvas, sums = frame_terms(positions, extended, probe, amplitudes)
    canvas = canvas[:, : tile_side + 2 * H]
    row_edges = jnp.concatenate([canvas[:, :H], canvas[:, tile_side + H :]], axis=1)
    from_rows = extended_2(row_edges, (("row", 1),), H)
    canvas = canvas.at[:, H : 2 * H].add(from_rows[:, :H])
    canvas = canvas.at[:, tile_side : tile_side + H].add(from_rows[:, 3 * H :])
    middle = canvas[:, H : tile_side + H]
    col_edges = jnp.concatenate([middle[:, :, :H], middle[:, :, tile_side + H :]], axis=2)
    from_cols = extended_2(col_edges, (("col", 2),), H)
    inner = middle[:, :, H : tile_side + H]
    inner = inner.at[:, :, :H].add(from_cols[:, :, :H])
    inner = inner.at[:, :, tile_side - H :].add(from_cols[:, :, 3 * H :])
    step_size = 1.0 / (jnp.max(jnp.sum(probe * probe, axis=(0, 1))) + 1e-06)
    new_object = object_field + inner * step_size
    total = total_over_mesh(sums)
    total = jnp.concatenate([total[0], total[1]], axis=-1)
    total_weight = total[-1]
    total_sum = total[:-1].reshape(probe.shape)
    new_probe = probe + (total_sum - probe * total_weight) / (total_weight + 1e-05)
    return (new_object, new_probe)


def solution(mesh):
    in_specs = (
        P("row", "col"),
        P("row", "col"),
        P(),
        P(("row", "col"), None, None),
        P(("row", "col"), None),
    )
    out_specs = (P(None, "row", "col"), P())
    return jax.shard_map(shards, mesh=mesh, in_specs=in_specs, out_specs=out_specs, check_vma=False)
```

```python
import functools
import math

import jax
import jax.numpy as jnp
from jax import lax
from jax.experimental import pallas as pl
from jax.experimental.pallas import tpu as pltpu
from jax.sharding import PartitionSpec as P

H = 64


def here():
    return {"row": lax.axis_index("row"), "col": lax.axis_index("col")}


def sides_of(axis, coords):
    count = lax.axis_size(axis)
    found = []
    for move in (-1, 1):
        other = dict(coords)
        other[axis] = lax.rem(coords[axis] + move + count, count)
        inside = coords[axis] > 0 if move < 0 else coords[axis] < count - 1
        found.append(((other["row"], other["col"]), inside))
    return found


def greet(devices):
    barrier = pltpu.get_barrier_semaphore()
    for device in devices:
        pl.semaphore_signal(barrier, inc=1, device_id=device, device_id_type=pl.DeviceIdType.MESH)
    pl.semaphore_wait(barrier, len(devices))


def swap_starts(axis, coords, copies):
    for (device, inside), copy in zip(sides_of(axis, coords), copies):

        @pl.when(inside)
        def _(copy=copy):
            copy.start()


def swap_waits(axis, coords, copies):
    for (device, inside), copy, back in zip(sides_of(axis, coords), copies, copies[::-1]):

        @pl.when(inside)
        def _(copy=copy, back=back):
            copy.wait_send()
            back.wait_recv()


def remote(source, target, send, recv, device):
    return pltpu.make_async_remote_copy(
        src_ref=source, dst_ref=target, send_sem=send, recv_sem=recv,
        device_id=device, device_id_type=pl.DeviceIdType.MESH,
    )


def edge_mask(shape):
    return lax.broadcasted_iota(jnp.int32, shape, 1) < H


def extend_kernel(tile_ref, ext_ref, edge, mid, from_cols, from_rows, send, recv):
    coords = here()
    side = tile_ref.shape[1]
    row_sides, col_sides = sides_of("row", coords), sides_of("col", coords)
    greet([device for device, _ in row_sides + col_sides])
    for c in range(2):
        edge[c] = pltpu.roll(tile_ref[c], H, axis=1)[:, : 2 * H]
    copies = [
        remote(edge, from_cols.at[1 - k], send.at[0, k], recv.at[0, k], col_sides[k][0])
        for k in range(2)
    ]
    swap_starts("col", coords, copies)
    swap_waits("col", coords, copies)
    step = 64
    has_low, has_high = col_sides[0][1], col_sides[1][1]
    for c in range(2):
        for r in range(0, side, step):
            rows = pl.ds(r, step)
            first = edge_mask((step, 2 * H))
            zero = jnp.zeros((step, 2 * H), jnp.float32)
            low = jnp.where(jnp.logical_and(first, has_low), from_cols[0, c, rows, :], zero)
            high = jnp.where(
                jnp.logical_and(jnp.logical_not(first), has_high), from_cols[1, c, rows, :], zero
            )
            rest = pltpu.roll(low + high, H, axis=1)
            line = pltpu.roll(jnp.concatenate([tile_ref[c, rows, :], rest], axis=1), H, axis=1)
            mid[c, rows, :] = line
            ext_ref[c, pl.ds(H + r, step), :] = line
    tops = [pl.ds(0, H), pl.ds(side - H, H)]
    copies = [
        remote(
            mid.at[:, tops[k], :], from_rows.at[1 - k], send.at[1, k], recv.at[1, k],
            row_sides[k][0],
        )
        for k in range(2)
    ]
    swap_starts("row", coords, copies)
    swap_waits("row", coords, copies)
    places = [0, side + H]
    for k in range(2):
        for c in range(2):
            got = from_rows[k, c]
            ext_ref[c, pl.ds(places[k], H), :] = jnp.where(
                row_sides[k][1], got, jnp.zeros_like(got)
            )
    for c in range(2):
        ext_ref[c, pl.ds(side + 2 * H, 8), :] = jnp.zeros((8, side + 2 * H), jnp.float32)


def extend(tile):
    side = tile.shape[1]
    wide = side + 2 * H
    f32 = jnp.float32
    dma = pltpu.SemaphoreType.DMA((2, 2))
    return pl.pallas_call(
        extend_kernel,
        out_shape=jax.ShapeDtypeStruct((2, wide + 8, wide), f32),
        in_specs=[pl.BlockSpec(memory_space=pltpu.VMEM)],
        out_specs=pl.BlockSpec(memory_space=pltpu.VMEM),
        scratch_shapes=[
            pltpu.VMEM((2, side, 2 * H), f32),
            pltpu.VMEM((2, side, wide), f32),
            pltpu.VMEM((2, 2, side, 2 * H), f32),
            pltpu.VMEM((2, 2, H, wide), f32),
            dma, dma,
        ],
        compiler_params=pltpu.CompilerParams(
            collective_id=1, has_side_effects=True, vmem_limit_bytes=16 * 1024 * 1024
        ),
        name="extend",
    )(tile)


def fourier_tables(side, sign):
    counter = jnp.arange(side, dtype=jnp.int32)
    product = counter[:, None] * counter[None, :] % side
    angle = product.astype(jnp.float32) * (2.0 * math.pi / side)
    norming = 1.0 / math.sqrt(side)
    real = (jnp.cos(angle) * norming).astype(jnp.bfloat16)
    imag = (sign * jnp.sin(angle) * norming).astype(jnp.bfloat16)
    left = jnp.concatenate(
        [jnp.concatenate([real, -imag], axis=1), jnp.concatenate([imag, real], axis=1)], axis=0
    )
    right = jnp.concatenate(
        [jnp.concatenate([real, imag], axis=1), jnp.concatenate([-imag, real], axis=1)], axis=0
    )
    return left, right


def dot(a, b):
    return jnp.dot(a, b, preferred_element_type=jnp.float32)


def frames_kernel(
    pos_ref, ext_ref, probe_ref, amp_ref, fl_ref, fr_ref, il_ref, ir_ref,
    canvas_ref, s_ref,
    o_scr, x_scr, h_scr, spec_scr, int_scr, p2_scr, g_scr,
):
    frame = pl.program_id(0)
    modes, _, n, _ = probe_ref.shape
    wide = ext_ref.shape[2]
    step = 32
    lanes = n // 2
    planes = 2 * modes

    def add_sum(plane, rows, value):
        s_ref[0, plane, rows, :] += value[:, :lanes]
        s_ref[1, plane, rows, :] += value[:, lanes:]

    chunks = [pl.ds(r, step) for r in range(0, n, step)]
    low = [pl.ds(n + r, step) for r in range(0, n, step)]

    @pl.when(frame == 0)
    def _():
        canvas_ref[...] = jnp.zeros_like(canvas_ref)
        s_ref[...] = jnp.zeros_like(s_ref)
        for rows in chunks:
            total = jnp.zeros((step, n), jnp.float32)
            for m in range(modes):
                for c in range(2):
                    total += probe_ref[m, c, rows, :] * probe_ref[m, c, rows, :]
            p2_scr[rows, :] = total

    r0 = pos_ref[frame, 0] + H
    c0 = pos_ref[frame, 1] + H
    base = pl.multiple_of(r0 // 8 * 8, 8)
    off = r0 - base
    tall = 64
    for r in range(0, n, tall):
        rows = pl.ds(r, tall)
        weight = jnp.zeros((tall, n), jnp.float32)
        for c in range(2):
            part = ext_ref[c, pl.ds(base + r, tall + 8), :]
            part = pltpu.roll(part, lax.rem(wide - c0, wide), axis=1)[:, :n]
            part = pltpu.roll(part, lax.rem(tall + 8 - off, tall + 8), axis=0)[:tall]
            o_scr[c, rows, :] = part
            weight += part * part
        add_sum(planes, rows, weight)

    for m in range(modes):
        for rows, under in zip(chunks, low):
            pr, pi = probe_ref[m, 0, rows, :], probe_ref[m, 1, rows, :]
            o_r, o_i = o_scr[0, rows, :], o_scr[1, rows, :]
            x_scr[m, rows, :] = (pr * o_r - pi * o_i).astype(jnp.bfloat16)
            x_scr[m, under, :] = (pr * o_i + pi * o_r).astype(jnp.bfloat16)
        half = dot(fl_ref[...], x_scr[m]).astype(jnp.bfloat16)
        h_scr[m, :, :n] = half[:n]
        h_scr[m, :, n:] = half[n:]
        spec_scr[m] = dot(h_scr[m], fr_ref[...])

    for rows in chunks:
        total = jnp.zeros((step, n), jnp.float32)
        for m in range(modes):
            a, b = spec_scr[m, rows, :n], spec_scr[m, rows, n:]
            total += a * a + b * b
        int_scr[rows, :] = amp_ref[0, rows, :] / jnp.maximum(jnp.sqrt(total), 1.0)

    for m in range(modes):
        for rows, under in zip(chunks, low):
            fac = int_scr[rows, :]
            x_scr[m, rows, :] = (spec_scr[m, rows, :n] * fac).astype(jnp.bfloat16)
            x_scr[m, under, :] = (spec_scr[m, rows, n:] * fac).astype(jnp.bfloat16)
        half = dot(il_ref[...], x_scr[m]).astype(jnp.bfloat16)
        h_scr[m, :, :n] = half[:n]
        h_scr[m, :, n:] = half[n:]
        spec_scr[m] = dot(h_scr[m], ir_ref[...])
        for rows in chunks:
            br, bi = spec_scr[m, rows, :n], spec_scr[m, rows, n:]
            o_r, o_i = o_scr[0, rows, :], o_scr[1, rows, :]
            pr, pi = probe_ref[m, 0, rows, :], probe_ref[m, 1, rows, :]
            add_sum(2 * m, rows, o_r * br + o_i * bi)
            add_sum(2 * m + 1, rows, o_r * bi - o_i * br)
            gr = pr * br + pi * bi
            gi = pr * bi - pi * br
            if m == 0:
                p2 = p2_scr[rows, :]
                gr -= o_r * p2
                gi -= o_i * p2
            else:
                gr += g_scr[0, rows, :]
                gi += g_scr[1, rows, :]
            g_scr[0, rows, :] = gr
            g_scr[1, rows, :] = gi

    for r in range(0, n, tall):
        for c in range(2):
            part = jnp.concatenate(
                [g_scr[c, pl.ds(r, tall), :], jnp.zeros((8, n), jnp.float32)], axis=0
            )
            part = pltpu.roll(part, off, axis=0)
            part = jnp.concatenate([part, jnp.zeros((tall + 8, wide - n), jnp.float32)], axis=1)
            canvas_ref[c, pl.ds(base + r, tall + 8), :] += pltpu.roll(part, c0, axis=1)


def frame_terms(positions, extended, probe, amplitudes):
    modes, _, n, _ = probe.shape
    frames = amplitudes.shape[0]
    wide = extended.shape[2]
    high = extended.shape[1]
    forward = fourier_tables(n, -1.0)
    inverse = fourier_tables(n, 1.0)
    f32 = jnp.float32
    sums = (2, 2 * modes + 1, n, n // 2)

    def whole(shape):
        return pl.BlockSpec(shape, lambda i, pos: (0,) * len(shape))

    return pl.pallas_call(
        frames_kernel,
        grid_spec=pltpu.PrefetchScalarGridSpec(
            num_scalar_prefetch=1,
            grid=(frames,),
            in_specs=[
                whole(extended.shape),
                whole(probe.shape),
                pl.BlockSpec((1, n, n), lambda i, pos: (i, 0, 0)),
            ]
            + [whole((2 * n, 2 * n))] * 4,
            out_specs=[whole((2, high, wide)), whole(sums)],
            scratch_shapes=[
                pltpu.VMEM((2, n, n), f32),
                pltpu.VMEM((modes, 2 * n, n), jnp.bfloat16),
                pltpu.VMEM((modes, n, 2 * n), jnp.bfloat16),
                pltpu.VMEM((modes, n, 2 * n), f32),
                pltpu.VMEM((n, n), f32),
                pltpu.VMEM((n, n), f32),
                pltpu.VMEM((2, n, n), f32),
            ],
        ),
        out_shape=[
            jax.ShapeDtypeStruct((2, high, wide), f32),
            jax.ShapeDtypeStruct(sums, f32),
        ],
        compiler_params=pltpu.CompilerParams(vmem_limit_bytes=48 * 1024 * 1024),
        name="frames",
    )(positions, extended, probe, amplitudes, *forward, *inverse)


def plan(sizes, rows):
    bits = [[(axis, b) for b in range(size.bit_length() - 1)] for axis, size in sizes]
    row_bits, col_bits = bits
    rest = col_bits[1:]
    cut = len(rest) // 2
    orders = [col_bits[:1] + rest + row_bits, col_bits[:1] + rest[cut:] + rest[:cut] + row_bits]
    plans = []
    for order in orders:
        left, stages, offset = rows, [], 0
        for axis, bit in order:
            halved = left > 8
            left = left // 2 if halved else left
            stages.append((axis, bit, halved, left, offset))
            offset += left
        plans.append(stages)
    return plans, max(stages[-1][3] + stages[-1][4] for stages in plans)


def total_kernel(
    plans, in_ref, canvas_ref, out_ref, inner_ref, partial, landed, send_rs, recv_rs, send_ag, recv_ag,
    mid, edge, from_cols, from_rows, send_halo, recv_halo,
):
    coords = here()

    def bit_of(axis, bit):
        return lax.rem(coords[axis] // (1 << bit), 2)

    def partner(axis, bit):
        flipped = dict(coords)
        flipped[axis] = coords[axis] + (1 - 2 * bit_of(axis, bit)) * (1 << bit)
        return (flipped["row"], flipped["col"])

    row_sides, col_sides = sides_of("row", coords), sides_of("col", coords)
    greet(
        [partner(axis, bit) for axis, bit, *_ in plans[0]]
        + [device for device, _ in row_sides + col_sides]
    )
    side = inner_ref.shape[1]
    places = [0, side + H]
    row_copies = [
        remote(
            canvas_ref.at[:, pl.ds(places[k], H), :], from_rows.at[1 - k],
            send_halo.at[0, k], recv_halo.at[0, k], row_sides[k][0],
        )
        for k in range(2)
    ]
    col_copies = [
        remote(edge, from_cols.at[1 - k], send_halo.at[1, k], recv_halo.at[1, k], col_sides[k][0])
        for k in range(2)
    ]

    def rows_done():
        swap_waits("row", coords, row_copies)
        for c in range(2):
            for r in range(0, side, H):
                part = canvas_ref[c, pl.ds(H + r, H), :]
                for k, at in ((0, 0), (1, side - H)):
                    if r == at:
                        got = from_rows[k, c]
                        part = part + jnp.where(row_sides[k][1], got, jnp.zeros_like(got))
                mid[c, pl.ds(r, H), :] = part
                edge[c, pl.ds(r, H), :] = pltpu.roll(part, H, axis=1)[:, : 2 * H]
        swap_starts("col", coords, col_copies)

    def cols_done():
        swap_waits("col", coords, col_copies)
        first = edge_mask((H, 2 * H))
        zero = jnp.zeros((H, 2 * H), jnp.float32)
        masks = [
            jnp.logical_and(first, col_sides[0][1]),
            jnp.logical_and(jnp.logical_not(first), col_sides[1][1]),
        ]
        for c in range(2):
            for r in range(0, side, H):
                rows = pl.ds(r, H)
                part = mid[c, rows, :]
                part = pltpu.roll(part, part.shape[1] - H, axis=1)[:, :side]
                pieces = []
                for k in range(2):
                    pieces.append(jnp.where(masks[k], from_cols[k, c, rows, :], zero))
                if side > 4 * H:
                    pieces.insert(1, jnp.zeros((H, side - 4 * H), jnp.float32))
                inner_ref[c, rows, :] = part + jnp.concatenate(pieces, axis=1)

    count = len(plans[0])
    starts = [[0], [0]]
    flights = [None, None]

    def send(part, stage):
        axis, bit, halved, size, offset = plans[part][stage]
        start = starts[part][-1]
        mine = bit_of(axis, bit)
        source = in_ref if stage == 0 else partial
        gone = pl.multiple_of(start + (1 - mine) * size, 8) if halved else start
        kept = pl.multiple_of(start + mine * size, 8) if halved else start
        starts[part].append(kept)
        copy = pltpu.make_async_remote_copy(
            src_ref=source.at[part, :, pl.ds(gone, size), :],
            dst_ref=landed.at[part, :, pl.ds(offset, size), :],
            send_sem=send_rs.at[part, stage],
            recv_sem=recv_rs.at[part, stage],
            device_id=partner(axis, bit),
            device_id_type=pl.DeviceIdType.MESH,
        )
        copy.start()
        flights[part] = copy

    def take(part, stage):
        _, _, _, size, offset = plans[part][stage]
        flights[part].wait()
        source = in_ref if stage == 0 else partial
        rows = pl.ds(starts[part][-1], size)
        target = out_ref if stage == count - 1 else partial
        target[part, :, rows, :] = (
            source[part, :, rows, :] + landed[part, :, pl.ds(offset, size), :]
        )

    def spread(part, stage):
        axis, bit, halved, size, _ = plans[part][stage]
        flights[part] = None
        if not halved:
            return
        rows = pl.ds(starts[part][stage + 1], size)
        copy = pltpu.make_async_remote_copy(
            src_ref=out_ref.at[part, :, rows, :],
            dst_ref=out_ref.at[part, :, rows, :],
            send_sem=send_ag.at[part, stage],
            recv_sem=recv_ag.at[part, stage],
            device_id=partner(axis, bit),
            device_id_type=pl.DeviceIdType.MESH,
        )
        copy.start()
        flights[part] = copy

    for part in range(2):
        send(part, 0)
    swap_starts("row", coords, row_copies)
    for stage in range(count):
        if stage == 1:
            rows_done()
        for part in range(2):
            take(part, stage)
            if stage + 1 < count:
                send(part, stage + 1)
            else:
                spread(part, stage)
    for stage in range(count - 2, -2, -1):
        for part in range(2):
            if flights[part] is not None:
                flights[part].wait()
            if stage >= 0:
                spread(part, stage)
        if stage == 0:
            cols_done()


def total_over_mesh(values, canvas):
    sizes = [(axis, lax.axis_size(axis)) for axis in ("row", "col")]
    parts, planes, rows, lanes = values.shape
    plans, landing = plan(sizes, rows)
    wide = canvas.shape[2]
    side = wide - 2 * H
    count = len(plans[0])
    dma = pltpu.SemaphoreType.DMA((parts, count))
    return pl.pallas_call(
        functools.partial(total_kernel, plans),
        out_shape=[
            jax.ShapeDtypeStruct(values.shape, values.dtype),
            jax.ShapeDtypeStruct((2, side, side), values.dtype),
        ],
        in_specs=[pl.BlockSpec(memory_space=pltpu.VMEM)] * 2,
        out_specs=[pl.BlockSpec(memory_space=pltpu.VMEM)] * 2,
        scratch_shapes=[
            pltpu.VMEM(values.shape, values.dtype),
            pltpu.VMEM((parts, planes, landing, lanes), values.dtype),
            dma, dma, dma, dma,
            pltpu.VMEM((2, side, wide), values.dtype),
            pltpu.VMEM((2, side, 2 * H), values.dtype),
            pltpu.VMEM((2, 2, side, 2 * H), values.dtype),
            pltpu.VMEM((2, 2, H, wide), values.dtype),
            pltpu.SemaphoreType.DMA((2, 2)),
            pltpu.SemaphoreType.DMA((2, 2)),
        ],
        compiler_params=pltpu.CompilerParams(
            collective_id=0, has_side_effects=True, vmem_limit_bytes=24 * 1024 * 1024
        ),
        name="total",
    )(values, canvas)


def shards(object_amplitude, object_phase, probe, amplitudes, positions):
    object_field = jnp.stack(
        [object_amplitude * jnp.cos(object_phase), object_amplitude * jnp.sin(object_phase)]
    )
    canvas, sums = frame_terms(positions, extend(object_field), probe, amplitudes)
    total, inner = total_over_mesh(sums, canvas)
    step_size = 1.0 / (jnp.max(jnp.sum(probe * probe, axis=(0, 1))) + 1e-06)
    new_object = object_field + inner * step_size
    total = jnp.concatenate([total[0], total[1]], axis=-1)
    total_weight = total[-1]
    total_sum = total[:-1].reshape(probe.shape)
    new_probe = probe + (total_sum - probe * total_weight) / (total_weight + 1e-05)
    return (new_object, new_probe)


def solution(mesh):
    in_specs = (
        P("row", "col"),
        P("row", "col"),
        P(),
        P(("row", "col"), None, None),
        P(("row", "col"), None),
    )
    out_specs = (P(None, "row", "col"), P())
    return jax.shard_map(shards, mesh=mesh, in_specs=in_specs, out_specs=out_specs, check_vma=False)
```

```python
import functools
import math

import jax
import jax.numpy as jnp
import numpy as np
from jax import lax
from jax.experimental import pallas as pl
from jax.experimental.pallas import tpu as pltpu
from jax.sharding import PartitionSpec as P

H = 64


def here():
    return {"row": lax.axis_index("row"), "col": lax.axis_index("col")}


def sides_of(axis, coords):
    count = lax.axis_size(axis)
    found = []
    for move in (-1, 1):
        other = dict(coords)
        other[axis] = lax.rem(coords[axis] + move + count, count)
        inside = coords[axis] > 0 if move < 0 else coords[axis] < count - 1
        found.append(((other["row"], other["col"]), inside))
    return found


def greet(devices):
    barrier = pltpu.get_barrier_semaphore()
    for device in devices:
        pl.semaphore_signal(barrier, inc=1, device_id=device, device_id_type=pl.DeviceIdType.MESH)
    pl.semaphore_wait(barrier, len(devices))


def swap_starts(axis, coords, copies):
    for (device, inside), copy in zip(sides_of(axis, coords), copies):

        @pl.when(inside)
        def _(copy=copy):
            copy.start()


def swap_waits(axis, coords, copies):
    for (device, inside), copy, back in zip(sides_of(axis, coords), copies, copies[::-1]):

        @pl.when(inside)
        def _(copy=copy, back=back):
            copy.wait_send()
            back.wait_recv()


def remote(source, target, send, recv, device):
    return pltpu.make_async_remote_copy(
        src_ref=source, dst_ref=target, send_sem=send, recv_sem=recv,
        device_id=device, device_id_type=pl.DeviceIdType.MESH,
    )


def edge_mask(shape):
    return lax.broadcasted_iota(jnp.int32, shape, 1) < H


def extend_kernel(tile_ref, ext_ref, edge, mid, from_cols, from_rows, send, recv):
    coords = here()
    side = tile_ref.shape[1]
    row_sides, col_sides = sides_of("row", coords), sides_of("col", coords)
    greet([device for device, _ in row_sides + col_sides])
    for c in range(2):
        edge[c] = pltpu.roll(tile_ref[c], H, axis=1)[:, : 2 * H]
    copies = [
        remote(edge, from_cols.at[1 - k], send.at[0, k], recv.at[0, k], col_sides[k][0])
        for k in range(2)
    ]
    swap_starts("col", coords, copies)
    swap_waits("col", coords, copies)
    step = 64
    has_low, has_high = col_sides[0][1], col_sides[1][1]
    for c in range(2):
        for r in range(0, side, step):
            rows = pl.ds(r, step)
            first = edge_mask((step, 2 * H))
            zero = jnp.zeros((step, 2 * H), jnp.float32)
            low = jnp.where(jnp.logical_and(first, has_low), from_cols[0, c, rows, :], zero)
            high = jnp.where(
                jnp.logical_and(jnp.logical_not(first), has_high), from_cols[1, c, rows, :], zero
            )
            rest = pltpu.roll(low + high, H, axis=1)
            line = pltpu.roll(jnp.concatenate([tile_ref[c, rows, :], rest], axis=1), H, axis=1)
            mid[c, rows, :] = line
            ext_ref[c, pl.ds(H + r, step), :] = line
    tops = [pl.ds(0, H), pl.ds(side - H, H)]
    copies = [
        remote(
            mid.at[:, tops[k], :], from_rows.at[1 - k], send.at[1, k], recv.at[1, k],
            row_sides[k][0],
        )
        for k in range(2)
    ]
    swap_starts("row", coords, copies)
    swap_waits("row", coords, copies)
    places = [0, side + H]
    for k in range(2):
        for c in range(2):
            got = from_rows[k, c]
            ext_ref[c, pl.ds(places[k], H), :] = jnp.where(
                row_sides[k][1], got, jnp.zeros_like(got)
            )
    for c in range(2):
        ext_ref[c, pl.ds(side + 2 * H, 8), :] = jnp.zeros((8, side + 2 * H), jnp.float32)


def extend(tile):
    side = tile.shape[1]
    wide = side + 2 * H
    f32 = jnp.float32
    dma = pltpu.SemaphoreType.DMA((2, 2))
    return pl.pallas_call(
        extend_kernel,
        out_shape=jax.ShapeDtypeStruct((2, wide + 8, wide), f32),
        in_specs=[pl.BlockSpec(memory_space=pltpu.VMEM)],
        out_specs=pl.BlockSpec(memory_space=pltpu.VMEM),
        scratch_shapes=[
            pltpu.VMEM((2, side, 2 * H), f32),
            pltpu.VMEM((2, side, wide), f32),
            pltpu.VMEM((2, 2, side, 2 * H), f32),
            pltpu.VMEM((2, 2, H, wide), f32),
            dma, dma,
        ],
        compiler_params=pltpu.CompilerParams(
            collective_id=1, has_side_effects=True, vmem_limit_bytes=16 * 1024 * 1024
        ),
        name="extend",
    )(tile)


def fourier_tables(side):
    counter = np.arange(side, dtype=np.int64)
    angle = (counter[:, None] * counter[None, :] % side) * (2.0 * math.pi / side)
    real = np.cos(angle) / math.sqrt(side)
    imag = -np.sin(angle) / math.sqrt(side)
    left = np.block([[real, -imag], [imag, real]])
    right = np.block([[real, imag], [-imag, real]])
    return [table.astype(np.float32).astype(jnp.bfloat16) for table in (left, right)]


def dot(a, b):
    return jnp.dot(a, b, preferred_element_type=jnp.float32)


def frames_kernel(
    pos_ref, ext_ref, probe_ref, amp_ref, left_ref, right_ref,
    canvas_ref, s_ref, step_ref,
    o_scr, x_scr, h_scr, spec_scr, int_scr, p2_scr, g_scr,
):
    frame = pl.program_id(0)
    modes, _, n, _ = probe_ref.shape
    wide = ext_ref.shape[2]
    step = 32
    lanes = n // 2
    planes = 2 * modes

    def add_sum(plane, rows, value):
        s_ref[0, plane, rows, :] += value[:, :lanes]
        s_ref[1, plane, rows, :] += value[:, lanes:]

    chunks = [pl.ds(r, step) for r in range(0, n, step)]
    low = [pl.ds(n + r, step) for r in range(0, n, step)]

    @pl.when(frame == 0)
    def _():
        canvas_ref[...] = jnp.zeros_like(canvas_ref)
        s_ref[...] = jnp.zeros_like(s_ref)
        for rows in chunks:
            total = jnp.zeros((step, n), jnp.float32)
            for m in range(modes):
                for c in range(2):
                    total += probe_ref[m, c, rows, :] * probe_ref[m, c, rows, :]
            p2_scr[rows, :] = total
        peak = jnp.max(jnp.max(p2_scr[...], axis=0, keepdims=True), axis=1, keepdims=True)
        step_ref[...] = jnp.broadcast_to(1.0 / (peak + 1e-06), step_ref.shape)

    r0 = pos_ref[frame, 0] + H
    c0 = pos_ref[frame, 1] + H
    base = pl.multiple_of(r0 // 8 * 8, 8)
    off = r0 - base
    tall = 64
    for r in range(0, n, tall):
        rows = pl.ds(r, tall)
        weight = jnp.zeros((tall, n), jnp.float32)
        for c in range(2):
            part = ext_ref[c, pl.ds(base + r, tall + 8), :]
            part = pltpu.roll(part, lax.rem(wide - c0, wide), axis=1)[:, :n]
            part = pltpu.roll(part, lax.rem(tall + 8 - off, tall + 8), axis=0)[:tall]
            o_scr[c, rows, :] = part
            weight += part * part
        add_sum(planes, rows, weight)

    for m in range(modes):
        for rows, under in zip(chunks, low):
            pr, pi = probe_ref[m, 0, rows, :], probe_ref[m, 1, rows, :]
            o_r, o_i = o_scr[0, rows, :], o_scr[1, rows, :]
            x_scr[m, rows, :] = (pr * o_r - pi * o_i).astype(jnp.bfloat16)
            x_scr[m, under, :] = (pr * o_i + pi * o_r).astype(jnp.bfloat16)
        half = dot(left_ref[...], x_scr[m]).astype(jnp.bfloat16)
        h_scr[m, :, :n] = half[:n]
        h_scr[m, :, n:] = half[n:]
        spec_scr[m] = dot(h_scr[m], right_ref[...])

    for rows in chunks:
        total = jnp.zeros((step, n), jnp.float32)
        for m in range(modes):
            a, b = spec_scr[m, rows, :n], spec_scr[m, rows, n:]
            total += a * a + b * b
        int_scr[rows, :] = amp_ref[0, rows, :] / jnp.maximum(jnp.sqrt(total), 1.0)

    for m in range(modes):
        for rows, under in zip(chunks, low):
            fac = int_scr[rows, :]
            x_scr[m, rows, :] = (spec_scr[m, rows, :n] * fac).astype(jnp.bfloat16)
            x_scr[m, under, :] = (spec_scr[m, rows, n:] * fac).astype(jnp.bfloat16)
        half = dot(right_ref[...], x_scr[m]).astype(jnp.bfloat16)
        h_scr[m, :, :n] = half[:n]
        h_scr[m, :, n:] = half[n:]
        spec_scr[m] = dot(h_scr[m], left_ref[...])
        for rows in chunks:
            br, bi = spec_scr[m, rows, :n], spec_scr[m, rows, n:]
            o_r, o_i = o_scr[0, rows, :], o_scr[1, rows, :]
            pr, pi = probe_ref[m, 0, rows, :], probe_ref[m, 1, rows, :]
            add_sum(2 * m, rows, o_r * br + o_i * bi)
            add_sum(2 * m + 1, rows, o_r * bi - o_i * br)
            gr = pr * br + pi * bi
            gi = pr * bi - pi * br
            if m == 0:
                p2 = p2_scr[rows, :]
                gr -= o_r * p2
                gi -= o_i * p2
            else:
                gr += g_scr[0, rows, :]
                gi += g_scr[1, rows, :]
            g_scr[0, rows, :] = gr
            g_scr[1, rows, :] = gi

    for r in range(0, n, tall):
        for c in range(2):
            part = jnp.concatenate(
                [g_scr[c, pl.ds(r, tall), :], jnp.zeros((8, n), jnp.float32)], axis=0
            )
            part = pltpu.roll(part, off, axis=0)
            part = jnp.concatenate([part, jnp.zeros((tall + 8, wide - n), jnp.float32)], axis=1)
            canvas_ref[c, pl.ds(base + r, tall + 8), :] += pltpu.roll(part, c0, axis=1)


def frame_terms(positions, extended, probe, amplitudes):
    modes, _, n, _ = probe.shape
    frames = amplitudes.shape[0]
    wide = extended.shape[2]
    high = extended.shape[1]
    tables = [jnp.asarray(table) for table in fourier_tables(n)]
    f32 = jnp.float32
    sums = (2, 2 * modes + 1, n, n // 2)

    def whole(shape):
        return pl.BlockSpec(shape, lambda i, pos: (0,) * len(shape))

    return pl.pallas_call(
        frames_kernel,
        grid_spec=pltpu.PrefetchScalarGridSpec(
            num_scalar_prefetch=1,
            grid=(frames,),
            in_specs=[
                whole(extended.shape),
                whole(probe.shape),
                pl.BlockSpec((1, n, n), lambda i, pos: (i, 0, 0)),
            ]
            + [whole((2 * n, 2 * n))] * 2,
            out_specs=[whole((2, high, wide)), whole(sums), whole((8, 128))],
            scratch_shapes=[
                pltpu.VMEM((2, n, n), f32),
                pltpu.VMEM((modes, 2 * n, n), jnp.bfloat16),
                pltpu.VMEM((modes, n, 2 * n), jnp.bfloat16),
                pltpu.VMEM((modes, n, 2 * n), f32),
                pltpu.VMEM((n, n), f32),
                pltpu.VMEM((n, n), f32),
                pltpu.VMEM((2, n, n), f32),
            ],
        ),
        out_shape=[
            jax.ShapeDtypeStruct((2, high, wide), f32),
            jax.ShapeDtypeStruct(sums, f32),
            jax.ShapeDtypeStruct((8, 128), f32),
        ],
        compiler_params=pltpu.CompilerParams(vmem_limit_bytes=48 * 1024 * 1024),
        name="frames",
    )(positions, extended, probe, amplitudes, *tables)


def plan(sizes, rows):
    bits = [[(axis, b) for b in range(size.bit_length() - 1)] for axis, size in sizes]
    row_bits, col_bits = bits
    rest = col_bits[1:]
    cut = len(rest) // 2
    orders = [col_bits[:1] + rest + row_bits, col_bits[:1] + rest[cut:] + rest[:cut] + row_bits]
    plans = []
    for order in orders:
        left, stages, offset = rows, [], 0
        for axis, bit in order:
            halved = left > 8
            left = left // 2 if halved else left
            stages.append((axis, bit, halved, left, offset))
            offset += left
        plans.append(stages)
    plans = plans * 2
    return plans, max(stages[-1][3] + stages[-1][4] for stages in plans)


def total_kernel(
    plans, in_ref, canvas_ref, out_ref, inner_ref, partial, landed, send_rs, recv_rs, send_ag, recv_ag,
    mid, edge, from_cols, from_rows, send_halo, recv_halo,
):
    coords = here()

    def bit_of(axis, bit):
        return lax.rem(coords[axis] // (1 << bit), 2)

    def partner(axis, bit):
        flipped = dict(coords)
        flipped[axis] = coords[axis] + (1 - 2 * bit_of(axis, bit)) * (1 << bit)
        return (flipped["row"], flipped["col"])

    row_sides, col_sides = sides_of("row", coords), sides_of("col", coords)
    greet(
        [partner(axis, bit) for axis, bit, *_ in plans[0]]
        + [device for device, _ in row_sides + col_sides]
    )
    side = inner_ref.shape[1]
    places = [0, side + H]
    row_copies = [
        remote(
            canvas_ref.at[:, pl.ds(places[k], H), :], from_rows.at[1 - k],
            send_halo.at[0, k], recv_halo.at[0, k], row_sides[k][0],
        )
        for k in range(2)
    ]
    col_copies = [
        remote(edge, from_cols.at[1 - k], send_halo.at[1, k], recv_halo.at[1, k], col_sides[k][0])
        for k in range(2)
    ]

    def rows_done():
        swap_waits("row", coords, row_copies)
        for c in range(2):
            for r in range(0, side, H):
                part = canvas_ref[c, pl.ds(H + r, H), :]
                for k, at in ((0, 0), (1, side - H)):
                    if r == at:
                        got = from_rows[k, c]
                        part = part + jnp.where(row_sides[k][1], got, jnp.zeros_like(got))
                mid[c, pl.ds(r, H), :] = part
                edge[c, pl.ds(r, H), :] = pltpu.roll(part, H, axis=1)[:, : 2 * H]
        swap_starts("col", coords, col_copies)

    def cols_done():
        swap_waits("col", coords, col_copies)
        first = edge_mask((H, 2 * H))
        zero = jnp.zeros((H, 2 * H), jnp.float32)
        masks = [
            jnp.logical_and(first, col_sides[0][1]),
            jnp.logical_and(jnp.logical_not(first), col_sides[1][1]),
        ]
        for c in range(2):
            for r in range(0, side, H):
                rows = pl.ds(r, H)
                part = mid[c, rows, :]
                part = pltpu.roll(part, part.shape[1] - H, axis=1)[:, :side]
                pieces = []
                for k in range(2):
                    pieces.append(jnp.where(masks[k], from_cols[k, c, rows, :], zero))
                if side > 4 * H:
                    pieces.insert(1, jnp.zeros((H, side - 4 * H), jnp.float32))
                inner_ref[c, rows, :] = part + jnp.concatenate(pieces, axis=1)

    count = len(plans[0])
    parts = len(plans)
    planes = in_ref.shape[1]
    cut = (planes + 1) // 2
    bands = [pl.ds(0, cut), pl.ds(0, cut), pl.ds(cut, planes - cut), pl.ds(cut, planes - cut)]
    starts = [[0] for _ in plans]
    flights = [None] * parts

    def send(part, stage):
        axis, bit, halved, size, offset = plans[part][stage]
        start = starts[part][-1]
        mine = bit_of(axis, bit)
        source = in_ref if stage == 0 else partial
        gone = pl.multiple_of(start + (1 - mine) * size, 8) if halved else start
        kept = pl.multiple_of(start + mine * size, 8) if halved else start
        starts[part].append(kept)
        copy = pltpu.make_async_remote_copy(
            src_ref=source.at[part % 2, bands[part], pl.ds(gone, size), :],
            dst_ref=landed.at[part % 2, bands[part], pl.ds(offset, size), :],
            send_sem=send_rs.at[part, stage],
            recv_sem=recv_rs.at[part, stage],
            device_id=partner(axis, bit),
            device_id_type=pl.DeviceIdType.MESH,
        )
        copy.start()
        flights[part] = copy

    def take(part, stage):
        _, _, _, size, offset = plans[part][stage]
        flights[part].wait()
        source = in_ref if stage == 0 else partial
        rows = pl.ds(starts[part][-1], size)
        target = out_ref if stage == count - 1 else partial
        half, band = part % 2, bands[part]
        target[half, band, rows, :] = (
            source[half, band, rows, :] + landed[half, band, pl.ds(offset, size), :]
        )

    def spread(part, stage):
        axis, bit, halved, size, _ = plans[part][stage]
        flights[part] = None
        if not halved:
            return
        rows = pl.ds(starts[part][stage + 1], size)
        copy = pltpu.make_async_remote_copy(
            src_ref=out_ref.at[part % 2, bands[part], rows, :],
            dst_ref=out_ref.at[part % 2, bands[part], rows, :],
            send_sem=send_ag.at[part, stage],
            recv_sem=recv_ag.at[part, stage],
            device_id=partner(axis, bit),
            device_id_type=pl.DeviceIdType.MESH,
        )
        copy.start()
        flights[part] = copy

    for part in range(parts):
        send(part, 0)
    swap_starts("row", coords, row_copies)
    for stage in range(count):
        if stage == 1:
            rows_done()
        for part in range(parts):
            take(part, stage)
            if stage + 1 < count:
                send(part, stage + 1)
            else:
                spread(part, stage)
    for stage in range(count - 2, -2, -1):
        for part in range(parts):
            if flights[part] is not None:
                flights[part].wait()
            if stage >= 0:
                spread(part, stage)
        if stage == 0:
            cols_done()


def total_over_mesh(values, canvas):
    sizes = [(axis, lax.axis_size(axis)) for axis in ("row", "col")]
    parts, planes, rows, lanes = values.shape
    plans, landing = plan(sizes, rows)
    wide = canvas.shape[2]
    side = wide - 2 * H
    count = len(plans[0])
    dma = pltpu.SemaphoreType.DMA((len(plans), count))
    return pl.pallas_call(
        functools.partial(total_kernel, plans),
        out_shape=[
            jax.ShapeDtypeStruct(values.shape, values.dtype),
            jax.ShapeDtypeStruct((2, side, side), values.dtype),
        ],
        in_specs=[pl.BlockSpec(memory_space=pltpu.VMEM)] * 2,
        out_specs=[pl.BlockSpec(memory_space=pltpu.VMEM)] * 2,
        scratch_shapes=[
            pltpu.VMEM(values.shape, values.dtype),
            pltpu.VMEM((parts, planes, landing, lanes), values.dtype),
            dma, dma, dma, dma,
            pltpu.VMEM((2, side, wide), values.dtype),
            pltpu.VMEM((2, side, 2 * H), values.dtype),
            pltpu.VMEM((2, 2, side, 2 * H), values.dtype),
            pltpu.VMEM((2, 2, H, wide), values.dtype),
            pltpu.SemaphoreType.DMA((2, 2)),
            pltpu.SemaphoreType.DMA((2, 2)),
        ],
        compiler_params=pltpu.CompilerParams(
            collective_id=0, has_side_effects=True, vmem_limit_bytes=24 * 1024 * 1024
        ),
        name="total",
    )(values, canvas)


def shards(object_amplitude, object_phase, probe, amplitudes, positions):
    object_field = jnp.stack(
        [object_amplitude * jnp.cos(object_phase), object_amplitude * jnp.sin(object_phase)]
    )
    canvas, sums, step_size = frame_terms(positions, extend(object_field), probe, amplitudes)
    total, inner = total_over_mesh(sums, canvas)
    new_object = object_field + inner * step_size[0, 0]
    total = jnp.concatenate([total[0], total[1]], axis=-1)
    total_weight = total[-1]
    total_sum = total[:-1].reshape(probe.shape)
    new_probe = probe + (total_sum - probe * total_weight) / (total_weight + 1e-05)
    return (new_object, new_probe)


def solution(mesh):
    in_specs = (
        P("row", "col"),
        P("row", "col"),
        P(),
        P(("row", "col"), None, None),
        P(("row", "col"), None),
    )
    out_specs = (P(None, "row", "col"), P())
    return jax.shard_map(shards, mesh=mesh, in_specs=in_specs, out_specs=out_specs, check_vma=False)
```

```python
import functools
import math

import jax
import jax.numpy as jnp
import numpy as np
from jax import lax
from jax.experimental import pallas as pl
from jax.experimental.pallas import tpu as pltpu
from jax.sharding import PartitionSpec as P

H = 64


def here():
    return {"row": lax.axis_index("row"), "col": lax.axis_index("col")}


def sides_of(axis, coords):
    count = lax.axis_size(axis)
    found = []
    for move in (-1, 1):
        other = dict(coords)
        other[axis] = lax.rem(coords[axis] + move + count, count)
        inside = coords[axis] > 0 if move < 0 else coords[axis] < count - 1
        found.append(((other["row"], other["col"]), inside))
    return found


def greet(devices):
    barrier = pltpu.get_barrier_semaphore()
    for device in devices:
        pl.semaphore_signal(barrier, inc=1, device_id=device, device_id_type=pl.DeviceIdType.MESH)
    pl.semaphore_wait(barrier, len(devices))


def swap_starts(axis, coords, copies):
    for (device, inside), copy in zip(sides_of(axis, coords), copies):

        @pl.when(inside)
        def _(copy=copy):
            copy.start()


def swap_waits(axis, coords, copies):
    for (device, inside), copy, back in zip(sides_of(axis, coords), copies, copies[::-1]):

        @pl.when(inside)
        def _(copy=copy, back=back):
            copy.wait_send()
            back.wait_recv()


def remote(source, target, send, recv, device):
    return pltpu.make_async_remote_copy(
        src_ref=source, dst_ref=target, send_sem=send, recv_sem=recv,
        device_id=device, device_id_type=pl.DeviceIdType.MESH,
    )


def edge_mask(shape):
    return lax.broadcasted_iota(jnp.int32, shape, 1) < H


def extend_kernel(tile_ref, ext_ref, edge, mid, from_cols, from_rows, send, recv):
    coords = here()
    side = tile_ref.shape[1]
    row_sides, col_sides = sides_of("row", coords), sides_of("col", coords)
    greet([device for device, _ in row_sides + col_sides])
    for c in range(2):
        edge[c] = pltpu.roll(tile_ref[c], H, axis=1)[:, : 2 * H]
    copies = [
        remote(edge, from_cols.at[1 - k], send.at[0, k], recv.at[0, k], col_sides[k][0])
        for k in range(2)
    ]
    swap_starts("col", coords, copies)
    swap_waits("col", coords, copies)
    step = 64
    has_low, has_high = col_sides[0][1], col_sides[1][1]
    for c in range(2):
        for r in range(0, side, step):
            rows = pl.ds(r, step)
            first = edge_mask((step, 2 * H))
            zero = jnp.zeros((step, 2 * H), jnp.float32)
            low = jnp.where(jnp.logical_and(first, has_low), from_cols[0, c, rows, :], zero)
            high = jnp.where(
                jnp.logical_and(jnp.logical_not(first), has_high), from_cols[1, c, rows, :], zero
            )
            rest = pltpu.roll(low + high, H, axis=1)
            line = pltpu.roll(jnp.concatenate([tile_ref[c, rows, :], rest], axis=1), H, axis=1)
            mid[c, rows, :] = line
            ext_ref[c, pl.ds(H + r, step), :] = line
    tops = [pl.ds(0, H), pl.ds(side - H, H)]
    copies = [
        remote(
            mid.at[:, tops[k], :], from_rows.at[1 - k], send.at[1, k], recv.at[1, k],
            row_sides[k][0],
        )
        for k in range(2)
    ]
    swap_starts("row", coords, copies)
    swap_waits("row", coords, copies)
    places = [0, side + H]
    for k in range(2):
        for c in range(2):
            got = from_rows[k, c]
            ext_ref[c, pl.ds(places[k], H), :] = jnp.where(
                row_sides[k][1], got, jnp.zeros_like(got)
            )
    for c in range(2):
        ext_ref[c, pl.ds(side + 2 * H, 8), :] = jnp.zeros((8, side + 2 * H), jnp.float32)


def extend(tile):
    side = tile.shape[1]
    wide = side + 2 * H
    f32 = jnp.float32
    dma = pltpu.SemaphoreType.DMA((2, 2))
    return pl.pallas_call(
        extend_kernel,
        out_shape=jax.ShapeDtypeStruct((2, wide + 8, wide), f32),
        in_specs=[pl.BlockSpec(memory_space=pltpu.VMEM)],
        out_specs=pl.BlockSpec(memory_space=pltpu.VMEM),
        scratch_shapes=[
            pltpu.VMEM((2, side, 2 * H), f32),
            pltpu.VMEM((2, side, wide), f32),
            pltpu.VMEM((2, 2, side, 2 * H), f32),
            pltpu.VMEM((2, 2, H, wide), f32),
            dma, dma,
        ],
        compiler_params=pltpu.CompilerParams(
            collective_id=1, has_side_effects=True, vmem_limit_bytes=16 * 1024 * 1024
        ),
        name="extend",
    )(tile)


def fourier_tables(side):
    counter = np.arange(side, dtype=np.int64)
    angle = (counter[:, None] * counter[None, :] % side) * (2.0 * math.pi / side)
    real = np.cos(angle) / math.sqrt(side)
    imag = -np.sin(angle) / math.sqrt(side)
    left = np.block([[real, -imag], [imag, real]])
    right = np.block([[real, imag], [-imag, real]])
    return [table.astype(np.float32).astype(jnp.bfloat16) for table in (left, right)]


def dot(a, b):
    return jnp.dot(a, b, preferred_element_type=jnp.float32)


def frames_kernel(
    pos_ref, ext_ref, probe_ref, amp_ref, left_ref, right_ref,
    canvas_ref, s_ref, step_ref,
    o_scr, x_scr, h_scr, spec_scr, int_scr, p2_scr, g_scr,
):
    frame = pl.program_id(0)
    modes, _, n, _ = probe_ref.shape
    wide = ext_ref.shape[2]
    step = 32
    lanes = n // 2
    planes = 2 * modes

    def add_sum(plane, rows, value):
        s_ref[0, plane, rows, :] += value[:, :lanes]
        s_ref[1, plane, rows, :] += value[:, lanes:]

    chunks = [pl.ds(r, step) for r in range(0, n, step)]
    low = [pl.ds(n + r, step) for r in range(0, n, step)]

    @pl.when(frame == 0)
    def _():
        canvas_ref[...] = jnp.zeros_like(canvas_ref)
        s_ref[...] = jnp.zeros_like(s_ref)
        for rows in chunks:
            total = jnp.zeros((step, n), jnp.float32)
            for m in range(modes):
                for c in range(2):
                    total += probe_ref[m, c, rows, :] * probe_ref[m, c, rows, :]
            p2_scr[rows, :] = total
        peak = jnp.max(jnp.max(p2_scr[...], axis=0, keepdims=True), axis=1, keepdims=True)
        step_ref[...] = jnp.broadcast_to(1.0 / (peak + 1e-06), step_ref.shape)

    r0 = pos_ref[frame, 0] + H
    c0 = pos_ref[frame, 1] + H
    base = pl.multiple_of(r0 // 8 * 8, 8)
    off = r0 - base
    tall = 64
    for r in range(0, n, tall):
        rows = pl.ds(r, tall)
        weight = jnp.zeros((tall, n), jnp.float32)
        for c in range(2):
            part = ext_ref[c, pl.ds(base + r, tall + 8), :]
            part = pltpu.roll(part, lax.rem(wide - c0, wide), axis=1)[:, :n]
            part = pltpu.roll(part, lax.rem(tall + 8 - off, tall + 8), axis=0)[:tall]
            o_scr[c, rows, :] = part
            weight += part * part
        add_sum(planes, rows, weight)

    for m in range(modes):
        for rows, under in zip(chunks, low):
            pr, pi = probe_ref[m, 0, rows, :], probe_ref[m, 1, rows, :]
            o_r, o_i = o_scr[0, rows, :], o_scr[1, rows, :]
            x_scr[m, rows, :] = (pr * o_r - pi * o_i).astype(jnp.bfloat16)
            x_scr[m, under, :] = (pr * o_i + pi * o_r).astype(jnp.bfloat16)
        half = dot(left_ref[...], x_scr[m]).astype(jnp.bfloat16)
        h_scr[m, :, :n] = half[:n]
        h_scr[m, :, n:] = half[n:]
        spec_scr[m] = dot(h_scr[m], right_ref[...])

    for rows in chunks:
        total = jnp.zeros((step, n), jnp.float32)
        for m in range(modes):
            a, b = spec_scr[m, rows, :n], spec_scr[m, rows, n:]
            total += a * a + b * b
        int_scr[rows, :] = amp_ref[0, rows, :] / jnp.maximum(jnp.sqrt(total), 1.0)

    for m in range(modes):
        for rows, under in zip(chunks, low):
            fac = int_scr[rows, :]
            x_scr[m, rows, :] = (spec_scr[m, rows, :n] * fac).astype(jnp.bfloat16)
            x_scr[m, under, :] = (spec_scr[m, rows, n:] * fac).astype(jnp.bfloat16)
        half = dot(right_ref[...], x_scr[m]).astype(jnp.bfloat16)
        h_scr[m, :, :n] = half[:n]
        h_scr[m, :, n:] = half[n:]
        spec_scr[m] = dot(h_scr[m], left_ref[...])
        for rows in chunks:
            br, bi = spec_scr[m, rows, :n], spec_scr[m, rows, n:]
            o_r, o_i = o_scr[0, rows, :], o_scr[1, rows, :]
            pr, pi = probe_ref[m, 0, rows, :], probe_ref[m, 1, rows, :]
            add_sum(2 * m, rows, o_r * br + o_i * bi)
            add_sum(2 * m + 1, rows, o_r * bi - o_i * br)
            gr = pr * br + pi * bi
            gi = pr * bi - pi * br
            if m == 0:
                p2 = p2_scr[rows, :]
                gr -= o_r * p2
                gi -= o_i * p2
            else:
                gr += g_scr[0, rows, :]
                gi += g_scr[1, rows, :]
            g_scr[0, rows, :] = gr
            g_scr[1, rows, :] = gi

    for r in range(0, n, tall):
        for c in range(2):
            part = jnp.concatenate(
                [g_scr[c, pl.ds(r, tall), :], jnp.zeros((8, n), jnp.float32)], axis=0
            )
            part = pltpu.roll(part, off, axis=0)
            part = jnp.concatenate([part, jnp.zeros((tall + 8, wide - n), jnp.float32)], axis=1)
            canvas_ref[c, pl.ds(base + r, tall + 8), :] += pltpu.roll(part, c0, axis=1)


def frame_terms(positions, extended, probe, amplitudes):
    modes, _, n, _ = probe.shape
    frames = amplitudes.shape[0]
    wide = extended.shape[2]
    high = extended.shape[1]
    tables = [jnp.asarray(table) for table in fourier_tables(n)]
    f32 = jnp.float32
    sums = (2, 2 * modes + 1, n, n // 2)

    def whole(shape):
        return pl.BlockSpec(shape, lambda i, pos: (0,) * len(shape))

    return pl.pallas_call(
        frames_kernel,
        grid_spec=pltpu.PrefetchScalarGridSpec(
            num_scalar_prefetch=1,
            grid=(frames,),
            in_specs=[
                whole(extended.shape),
                whole(probe.shape),
                pl.BlockSpec((1, n, n), lambda i, pos: (i, 0, 0)),
            ]
            + [whole((2 * n, 2 * n))] * 2,
            out_specs=[whole((2, high, wide)), whole(sums), whole((8, 128))],
            scratch_shapes=[
                pltpu.VMEM((2, n, n), f32),
                pltpu.VMEM((modes, 2 * n, n), jnp.bfloat16),
                pltpu.VMEM((modes, n, 2 * n), jnp.bfloat16),
                pltpu.VMEM((modes, n, 2 * n), f32),
                pltpu.VMEM((n, n), f32),
                pltpu.VMEM((n, n), f32),
                pltpu.VMEM((2, n, n), f32),
            ],
        ),
        out_shape=[
            jax.ShapeDtypeStruct((2, high, wide), f32),
            jax.ShapeDtypeStruct(sums, f32),
            jax.ShapeDtypeStruct((8, 128), f32),
        ],
        compiler_params=pltpu.CompilerParams(vmem_limit_bytes=48 * 1024 * 1024),
        name="frames",
    )(positions, extended, probe, amplitudes, *tables)


def plan(sizes, rows):
    bits = [[(axis, b) for b in range(size.bit_length() - 1)] for axis, size in sizes]
    row_bits, col_bits = bits
    rest = col_bits[1:]
    cut = len(rest) // 2
    orders = [col_bits[:1] + rest + row_bits, col_bits[:1] + rest[cut:] + rest[:cut] + row_bits]
    plans = []
    for order in orders:
        left, stages, offset = rows, [], 0
        for axis, bit in order:
            halved = left > 8
            left = left // 2 if halved else left
            stages.append((axis, bit, halved, left, offset))
            offset += left
        plans.append(stages)
    plans = plans * 3
    return plans, max(stages[-1][3] + stages[-1][4] for stages in plans)


def total_kernel(
    plans, in_ref, canvas_ref, out_ref, inner_ref, partial, landed, send_rs, recv_rs, send_ag, recv_ag,
    mid, edge, from_cols, from_rows, send_halo, recv_halo,
):
    coords = here()

    def bit_of(axis, bit):
        return lax.rem(coords[axis] // (1 << bit), 2)

    def partner(axis, bit):
        flipped = dict(coords)
        flipped[axis] = coords[axis] + (1 - 2 * bit_of(axis, bit)) * (1 << bit)
        return (flipped["row"], flipped["col"])

    row_sides, col_sides = sides_of("row", coords), sides_of("col", coords)
    greet(
        [partner(axis, bit) for axis, bit, *_ in plans[0]]
        + [device for device, _ in row_sides + col_sides]
    )
    side = inner_ref.shape[1]
    places = [0, side + H]
    row_copies = [
        remote(
            canvas_ref.at[:, pl.ds(places[k], H), :], from_rows.at[1 - k],
            send_halo.at[0, k], recv_halo.at[0, k], row_sides[k][0],
        )
        for k in range(2)
    ]
    col_copies = [
        remote(edge, from_cols.at[1 - k], send_halo.at[1, k], recv_halo.at[1, k], col_sides[k][0])
        for k in range(2)
    ]

    def rows_done():
        swap_waits("row", coords, row_copies)
        for c in range(2):
            for r in range(0, side, H):
                part = canvas_ref[c, pl.ds(H + r, H), :]
                for k, at in ((0, 0), (1, side - H)):
                    if r == at:
                        got = from_rows[k, c]
                        part = part + jnp.where(row_sides[k][1], got, jnp.zeros_like(got))
                mid[c, pl.ds(r, H), :] = part
                edge[c, pl.ds(r, H), :] = pltpu.roll(part, H, axis=1)[:, : 2 * H]
        swap_starts("col", coords, col_copies)

    def cols_done():
        swap_waits("col", coords, col_copies)
        first = edge_mask((H, 2 * H))
        zero = jnp.zeros((H, 2 * H), jnp.float32)
        masks = [
            jnp.logical_and(first, col_sides[0][1]),
            jnp.logical_and(jnp.logical_not(first), col_sides[1][1]),
        ]
        for c in range(2):
            for r in range(0, side, H):
                rows = pl.ds(r, H)
                part = mid[c, rows, :]
                part = pltpu.roll(part, part.shape[1] - H, axis=1)[:, :side]
                pieces = []
                for k in range(2):
                    pieces.append(jnp.where(masks[k], from_cols[k, c, rows, :], zero))
                if side > 4 * H:
                    pieces.insert(1, jnp.zeros((H, side - 4 * H), jnp.float32))
                inner_ref[c, rows, :] = part + jnp.concatenate(pieces, axis=1)

    count = len(plans[0])
    parts = len(plans)
    planes = in_ref.shape[1]
    cuts = [planes * k // 3 for k in range(4)]
    bands = [pl.ds(cuts[p // 2], cuts[p // 2 + 1] - cuts[p // 2]) for p in range(parts)]
    starts = [[0] for _ in plans]
    flights = [None] * parts

    def send(part, stage):
        axis, bit, halved, size, offset = plans[part][stage]
        start = starts[part][-1]
        mine = bit_of(axis, bit)
        source = in_ref if stage == 0 else partial
        gone = pl.multiple_of(start + (1 - mine) * size, 8) if halved else start
        kept = pl.multiple_of(start + mine * size, 8) if halved else start
        starts[part].append(kept)
        copy = pltpu.make_async_remote_copy(
            src_ref=source.at[part % 2, bands[part], pl.ds(gone, size), :],
            dst_ref=landed.at[part % 2, bands[part], pl.ds(offset, size), :],
            send_sem=send_rs.at[part, stage],
            recv_sem=recv_rs.at[part, stage],
            device_id=partner(axis, bit),
            device_id_type=pl.DeviceIdType.MESH,
        )
        copy.start()
        flights[part] = copy

    def take(part, stage):
        _, _, _, size, offset = plans[part][stage]
        flights[part].wait()
        source = in_ref if stage == 0 else partial
        rows = pl.ds(starts[part][-1], size)
        target = out_ref if stage == count - 1 else partial
        half, band = part % 2, bands[part]
        target[half, band, rows, :] = (
            source[half, band, rows, :] + landed[half, band, pl.ds(offset, size), :]
        )

    def spread(part, stage):
        axis, bit, halved, size, _ = plans[part][stage]
        flights[part] = None
        if not halved:
            return
        rows = pl.ds(starts[part][stage + 1], size)
        copy = pltpu.make_async_remote_copy(
            src_ref=out_ref.at[part % 2, bands[part], rows, :],
            dst_ref=out_ref.at[part % 2, bands[part], rows, :],
            send_sem=send_ag.at[part, stage],
            recv_sem=recv_ag.at[part, stage],
            device_id=partner(axis, bit),
            device_id_type=pl.DeviceIdType.MESH,
        )
        copy.start()
        flights[part] = copy

    for part in range(parts):
        send(part, 0)
    swap_starts("row", coords, row_copies)
    for stage in range(count):
        if stage == 1:
            rows_done()
        for part in range(parts):
            take(part, stage)
            if stage + 1 < count:
                send(part, stage + 1)
            else:
                spread(part, stage)
    for stage in range(count - 2, -2, -1):
        for part in range(parts):
            if flights[part] is not None:
                flights[part].wait()
            if stage >= 0:
                spread(part, stage)
        if stage == 0:
            cols_done()


def total_over_mesh(values, canvas):
    sizes = [(axis, lax.axis_size(axis)) for axis in ("row", "col")]
    parts, planes, rows, lanes = values.shape
    plans, landing = plan(sizes, rows)
    wide = canvas.shape[2]
    side = wide - 2 * H
    count = len(plans[0])
    dma = pltpu.SemaphoreType.DMA((len(plans), count))
    return pl.pallas_call(
        functools.partial(total_kernel, plans),
        out_shape=[
            jax.ShapeDtypeStruct(values.shape, values.dtype),
            jax.ShapeDtypeStruct((2, side, side), values.dtype),
        ],
        in_specs=[pl.BlockSpec(memory_space=pltpu.VMEM)] * 2,
        out_specs=[pl.BlockSpec(memory_space=pltpu.VMEM)] * 2,
        scratch_shapes=[
            pltpu.VMEM(values.shape, values.dtype),
            pltpu.VMEM((parts, planes, landing, lanes), values.dtype),
            dma, dma, dma, dma,
            pltpu.VMEM((2, side, wide), values.dtype),
            pltpu.VMEM((2, side, 2 * H), values.dtype),
            pltpu.VMEM((2, 2, side, 2 * H), values.dtype),
            pltpu.VMEM((2, 2, H, wide), values.dtype),
            pltpu.SemaphoreType.DMA((2, 2)),
            pltpu.SemaphoreType.DMA((2, 2)),
        ],
        compiler_params=pltpu.CompilerParams(
            collective_id=0, has_side_effects=True, vmem_limit_bytes=24 * 1024 * 1024
        ),
        name="total",
    )(values, canvas)


def shards(object_amplitude, object_phase, probe, amplitudes, positions):
    object_field = jnp.stack(
        [object_amplitude * jnp.cos(object_phase), object_amplitude * jnp.sin(object_phase)]
    )
    canvas, sums, step_size = frame_terms(positions, extend(object_field), probe, amplitudes)
    total, inner = total_over_mesh(sums, canvas)
    new_object = object_field + inner * step_size[0, 0]
    total = jnp.concatenate([total[0], total[1]], axis=-1)
    total_weight = total[-1]
    total_sum = total[:-1].reshape(probe.shape)
    new_probe = probe + (total_sum - probe * total_weight) / (total_weight + 1e-05)
    return (new_object, new_probe)


def solution(mesh):
    in_specs = (
        P("row", "col"),
        P("row", "col"),
        P(),
        P(("row", "col"), None, None),
        P(("row", "col"), None),
    )
    out_specs = (P(None, "row", "col"), P())
    return jax.shard_map(shards, mesh=mesh, in_specs=in_specs, out_specs=out_specs, check_vma=False)
```
